32 devices in a mesh: node: 8 (over y, x, core), freq: 4 (over z).
Axes of the slice: x: 2, y: 2, z: 4, core: 2. Of those that a mesh axis runs over, the one named last changes fastest.
Arguments:
- density: float32 [256, 16, 2048], P('freq', None, 'node'), may hold values from -6 to 6
- coords: float32 [3, 2048], P(None, 'node'), may hold values from -4 to 4
- weights: float32 [2048], P('node'), may hold values from 0.1 to 1
- neighbours: int32 [16, 4], P('node'), may hold values from 0 to 15, as said below
- counts: int32 [16], P('node'), may hold values from 1 to 4, as said below
Outputs:
- field: float32 [256, 16, 2048], P('freq', None, 'node')
The draws below stay inside these ranges and needn't reach their ends.
Inputs may be any that keep to these rules, and one draw needn't show every extreme that they name: `neighbours`: row p starts with p itself, then lists distinct patches that lie within 2 places of p in the cyclic order of patches; only the first counts[p] entries of a row are used, the rest are valid patch numbers. `counts`: some patch uses all 4 entries.
All inputs are finite; a program needn't handle non-finite values.
Results may differ from the reference program's by a relative error of at most 0.0003.
Values sent between devices are 32-bit elements; how exact they have to be, the bound alone decides.
No kernel may reach another device: no remote copies, remote signals or barrier semaphores. Data moves between devices by JAX's collectives and lax.ppermute only.
A program may use at most 64 MiB of HBM per device.

```python
import math
import jax
import jax.numpy as jnp
from jax import lax

STEPS = 256
FIELDS = 16
PATCH = 128
PATCH_DEV = 2
NEAR_MOST = 4
PATCHES = 16
NODES = 2048


def adjacency_helper(key):
    base_key = jax.random.fold_in(key, 7)
    count_key, force_key, order_key = jax.random.split(base_key, 3)
    live_counts = jax.random.randint(count_key, (PATCHES,), 1, NEAR_MOST + 1)
    chosen = jax.random.randint(force_key, (), 0, PATCHES)
    live_counts = jnp.where(jnp.arange(PATCHES) == chosen, NEAR_MOST, live_counts)
    span_size = 2 * PATCH_DEV
    scores = jax.random.randint(order_key, (PATCHES, span_size), 0, 1 << 20) * span_size + jnp.arange(span_size)[None, :]
    ordering = jnp.argsort(scores, axis=1)
    offsets = jnp.where(ordering < PATCH_DEV, ordering - PATCH_DEV, ordering - PATCH_DEV + 1)
    picked = offsets[:, :NEAR_MOST - 1]
    own_patch = jnp.arange(PATCHES)[:, None]
    listing = jnp.concatenate([own_patch, (own_patch + picked) % PATCHES], axis=1)
    return (listing.astype(jnp.int32), live_counts.astype(jnp.int32))


def draw_neighbours(key, part):
    listing, live_counts = adjacency_helper(key)
    return listing


def draw_counts(key, part):
    listing, live_counts = adjacency_helper(key)
    return live_counts


def draw_coords(key, part):
    jitter_key = jax.random.fold_in(key, 11)
    patch_ids = (jnp.arange(NODES) // PATCH).astype(jnp.float32)
    phase_angle = 2.0 * jnp.pi * patch_ids / PATCHES
    radius = PATCHES / (2.0 * jnp.pi)
    centres = jnp.stack([radius * jnp.cos(phase_angle), radius * jnp.sin(phase_angle), jnp.zeros_like(phase_angle)])
    jitter = jax.random.uniform(jitter_key, (3, NODES), jnp.float32, -0.5, 0.5)
    return (centres + jitter).astype(jnp.float32)


def levels(rng, shape, pieces, low, top_value):
    factor_of = 1.0
    for position, blocks in pieces:
        draws = jax.random.uniform(jax.random.fold_in(jax.random.fold_in(rng, 6), position), (blocks,), jnp.float32, low / len(pieces), top_value / len(pieces))
        factor_of = factor_of * jnp.repeat(jnp.exp(draws), shape[position] // blocks).reshape((-1,) + (1,) * (len(shape) - 1 - position))
    return factor_of


def bell_draw(key, extent, spread, bound, cuts=(), kind=jnp.bfloat16):
    array = spread * jax.random.normal(key, extent, jnp.float32)
    if cuts:
        array = array * levels(key, extent, cuts, -0.22, 0.18)
    return jnp.clip(array, -bound, bound).astype(kind)


def setup_inputs(seed: int = 0) -> dict:
    key_of = jax.random.split(jax.random.key(seed), 6)
    density = bell_draw(key_of[0], (STEPS, FIELDS, NODES), 1.0, 6.0, ((0, 4), (2, 8)), jnp.float32)
    coords = draw_coords(jax.random.fold_in(key_of[5], 71), 0)
    weights = jnp.clip(jnp.exp(math.log(1.0) - 2.3025851 * jax.random.uniform(key_of[2], (NODES,), jnp.float32) ** levels(key_of[2], (NODES,), ((0, 8),), -0.2, 0.2)), 0.1, 1.0)
    neighbours = draw_neighbours(jax.random.fold_in(key_of[5], 71), 0)
    counts = draw_counts(jax.random.fold_in(key_of[5], 71), 0)
    return dict(density=density, coords=coords, weights=weights, neighbours=neighbours, counts=counts)


decay_ratio = 0.1
time_step = 1.0
smoothing = 0.5
highest = lax.Precision.HIGHEST

def fourier_tables(freq_count):
    freq_index = jnp.arange(freq_count, dtype=jnp.int32)
    time_index = jnp.arange(STEPS, dtype=jnp.int32)
    phase_index = (2 * freq_index[:, None] + 1) * time_index[None, :] % (2 * STEPS)
    phase_angle = phase_index.astype(jnp.float32) * (jnp.pi / STEPS)
    return (jnp.cos(phase_angle), jnp.sin(phase_angle))

def laplace_values(freq_index):
    phase_angle = (2 * freq_index + 1).astype(jnp.float32) * (jnp.pi / STEPS)
    radius = decay_ratio ** (1.0 / STEPS)
    offset_real = 1.0 - radius * jnp.cos(phase_angle)
    offset_imag = -radius * jnp.sin(phase_angle)
    delta_real = offset_real + 0.5 * (offset_real * offset_real - offset_imag * offset_imag)
    delta_imag = offset_imag + offset_real * offset_imag
    return (delta_real / time_step, delta_imag / time_step)

def time_weights(time_index, sign):
    radius = decay_ratio ** (1.0 / STEPS)
    return jnp.power(jnp.float32(radius), sign * time_index.astype(jnp.float32))

def kernel_terms(distance, static_part, value_real, value_imag):
    decaying = jnp.exp(-value_real * distance) * static_part
    return (decaying * jnp.cos(value_imag * distance), -decaying * jnp.sin(value_imag * distance))

def reference(density, coords, weights, neighbours, counts):
    half_count = STEPS // 2
    cosine, sine = fourier_tables(half_count)
    time_index = jnp.arange(STEPS, dtype=jnp.int32)
    scaled = density * time_weights(time_index, 1.0)[:, None, None]
    flattened = scaled.reshape(STEPS, FIELDS * NODES)
    spec_real = jnp.dot(cosine, flattened, precision=highest, preferred_element_type=jnp.float32).reshape(half_count, FIELDS, NODES)
    spec_imag = jnp.dot(sine, flattened, precision=highest, preferred_element_type=jnp.float32).reshape(half_count, FIELDS, NODES)
    laplace_real, laplace_imag = laplace_values(jnp.arange(half_count, dtype=jnp.int32))
    slot_index = jnp.arange(NEAR_MOST, dtype=jnp.int32)
    node_offset = jnp.arange(PATCH, dtype=jnp.int32)

    def one_patch(patch_index):
        own_coords = lax.dynamic_slice_in_dim(coords, patch_index * PATCH, PATCH, 1)
        columns = (neighbours[patch_index][:, None] * PATCH + node_offset[None, :]).reshape(NEAR_MOST * PATCH)
        other_coords = coords[:, columns]
        live_slots = (slot_index < counts[patch_index]).astype(jnp.float32)
        node_scale = weights[columns] * jnp.repeat(live_slots, PATCH)
        separation = own_coords[:, :, None] - other_coords[:, None, :]
        distance = jnp.sqrt(lax.optimization_barrier(jnp.sum(separation * separation, axis=0)) + smoothing * smoothing)
        static_part = node_scale[None, :] / (4.0 * jnp.pi * distance)
        near_real = spec_real[:, :, columns]
        near_imag = spec_imag[:, :, columns]
        kern_real, kern_imag = kernel_terms(distance[None], static_part[None], laplace_real[:, None, None], laplace_imag[:, None, None])
        out_real = jnp.einsum('fij,frj->fri', kern_real, near_real, precision=highest) - jnp.einsum('fij,frj->fri', kern_imag, near_imag, precision=highest)
        out_imag = jnp.einsum('fij,frj->fri', kern_real, near_imag, precision=highest) + jnp.einsum('fij,frj->fri', kern_imag, near_real, precision=highest)
        return (out_real, out_imag)
    result_real, result_imag = lax.map(one_patch, jnp.arange(PATCHES, dtype=jnp.int32))
    result_real = jnp.transpose(result_real, (1, 2, 0, 3)).reshape(half_count, FIELDS * NODES)
    result_imag = jnp.transpose(result_imag, (1, 2, 0, 3)).reshape(half_count, FIELDS * NODES)
    summed = jnp.dot(cosine.T, result_real, precision=highest, preferred_element_type=jnp.float32) + jnp.dot(sine.T, result_imag, precision=highest, preferred_element_type=jnp.float32)
    summed = summed * (2.0 / STEPS) * time_weights(time_index, -1.0)[:, None]
    return summed.reshape(STEPS, FIELDS, NODES)
```

```python
import functools

import jax
import jax.numpy as jnp
import numpy as np
from jax import lax
from jax.experimental import pallas as pl
from jax.experimental.pallas import tpu as pltpu
from jax.sharding import PartitionSpec as P

STEPS = 256
PATCH = 128
PATCH_DEV = 2
NEAR_MOST = 4

decay_ratio = 0.1
time_step = 1.0
smoothing = 0.5
highest = lax.Precision.HIGHEST

UNROLL = 8
f32 = jnp.float32
bf16 = jnp.bfloat16


def angles(freqs, times):
    phase = (2 * freqs[:, None] + 1) * times[None, :] % (2 * STEPS)
    return phase * (np.pi / STEPS)


def forward_table():
    times = np.arange(STEPS)
    angle = angles(np.arange(STEPS // 2), times)
    rows = np.stack([np.cos(angle), np.sin(angle)], axis=1).reshape(STEPS, STEPS)
    return (rows * decay_ratio ** (times / STEPS)).T.astype(np.float32)


def inverse_table():
    times = np.arange(STEPS)
    angle = angles(np.arange(STEPS // 2), times)
    rows = np.stack([np.cos(angle), np.sin(angle)], axis=1).reshape(STEPS, STEPS)
    return (rows.T * (2.0 / STEPS) * decay_ratio ** (-times[:, None] / STEPS)).astype(np.float32)


def laplace_table():
    zeta = decay_ratio ** (1.0 / STEPS) * np.exp(1j * np.pi * (2 * np.arange(STEPS // 2) + 1) / STEPS)
    value = ((1 - zeta) + (1 - zeta) ** 2 / 2) / time_step
    return (
        (-value.real / np.log(2.0)).astype(np.float32),
        (value.imag / (2 * np.pi)).astype(np.float32),
    )


def trig_series():
    w = 0.125 * (1 - np.cos(np.pi * (np.arange(4000) + 0.5) / 4000))

    def fit(values):
        basis = np.polynomial.chebyshev.chebvander(w * 8 - 1, 4)
        found = np.linalg.lstsq(basis, values, rcond=None)[0]
        series = np.polynomial.chebyshev.Chebyshev(found, domain=[0, 0.25])
        return [float(np.float32(c)) for c in series.convert(kind=np.polynomial.Polynomial).coef]

    root = np.sqrt(w)
    return (
        fit(np.sqrt(2.0) * np.sin(np.pi * root) / root),
        fit(np.sqrt(2.0) * np.cos(np.pi * root)),
    )


SINE, COSINE = trig_series()


def series(terms, w):
    total = terms[-1] * w + terms[-2]
    for term in terms[-3::-1]:
        total = total * w + term
    return total


def split(x):
    high = x.astype(bf16)
    return high, (x - high.astype(f32)).astype(bf16)


def dot(a, b):
    return jnp.dot(a, b, preferred_element_type=f32)


def dot3(a, b):
    (a_high, a_low), (b_high, b_low) = a, b
    return dot(a_high, b_high) + (dot(a_high, b_low) + dot(a_low, b_high))


def kernel_value(r, static_part, rate, turns):
    t = r * turns
    u = t - jnp.round(t)
    w = u * u
    s = series(SINE, w) * u
    c = series(COSINE, w)
    e = jnp.exp2(r * rate) * static_part
    es = e * s
    return e - es * s, -(es * c)


VMEM = pl.BlockSpec(memory_space=pltpu.VMEM)
SMEM = pl.BlockSpec(memory_space=pltpu.SMEM)
ANY = pl.BlockSpec(memory_space=pl.ANY)


def call(body, name, outs, ins, specs, out_specs=None, scratch=(), flops=0, moved=0, trans=0):
    return pl.pallas_call(
        body,
        name=name,
        out_shape=outs,
        in_specs=specs,
        out_specs=out_specs if out_specs is not None else jax.tree.map(lambda _: VMEM, outs),
        scratch_shapes=list(scratch),
        cost_estimate=pl.CostEstimate(flops=flops, bytes_accessed=moved, transcendentals=trans),
    )(*ins)


def shape(*dims, dtype=f32):
    return jax.ShapeDtypeStruct(dims, dtype)


def pack_body(parts, fields, where, x_ref, *outs):
    times = x_ref.shape[0]
    for step, out in enumerate(outs):
        group = lax.rem(where[0] + step, parts)
        field0 = pl.multiple_of(group // 2 * fields, 8)
        node0 = pl.multiple_of(group % 2 * PATCH, PATCH)
        block = x_ref[:, pl.ds(field0, fields), pl.ds(node0, PATCH)]
        out[...] = block.reshape(times * fields, PATCH)


def unpack_body(parts, fields, where, *refs):
    out = refs[-1]
    times = out.shape[0]
    for step, ref in enumerate(refs[:-1]):
        group = lax.rem(where[0] + parts - step, parts)
        field0 = pl.multiple_of(group // 2 * fields, 8)
        node0 = pl.multiple_of(group % 2 * PATCH, PATCH)
        out[:, pl.ds(field0, fields), pl.ds(node0, PATCH)] = ref[...].reshape(times, fields, PATCH)


def forward_body(parts, fields, where, table, weights, *refs):
    blocks, (own, other) = refs[:parts], refs[parts:]
    times = STEPS // parts
    half = STEPS // 2
    part = where[0]
    rows = jnp.concatenate(
        [table[lax.rem(part + parts - step, parts)] for step in range(parts)], axis=1
    )
    low_half = where[1] == 0
    first = jnp.where(low_half, rows[0], rows[1])
    second = jnp.where(low_half, rows[1], rows[0])
    matrix = split(jnp.concatenate([first, second], axis=1).T)
    for field in range(0, fields, 2):
        pair = [
            jnp.concatenate([b[pl.ds(f, times, stride=fields), :] for b in blocks], axis=0)
            for f in (field, field + 1)
        ]
        result = dot3(matrix, split(jnp.concatenate(pair, axis=1)))
        for i in range(2):
            column = result[:, i * PATCH : (i + 1) * PATCH] * weights[...]
            own[pl.ds(field + i, half, stride=fields), :] = column[:half]
            other[pl.ds(field + i, half, stride=fields), :] = column[half:]


def inverse_body(parts, fields, where, table, own, other, *outs):
    times = STEPS // parts
    half = STEPS // 2
    low_half = where[1] == 0
    matrices = []
    for step in range(parts):
        rows = table[lax.rem(where[0] + step, parts)]
        first = jnp.where(low_half, rows[0], rows[1])
        second = jnp.where(low_half, rows[1], rows[0])
        matrices.append(jnp.concatenate([first, second], axis=1))
    matrix = split(jnp.concatenate(matrices, axis=0))
    for field in range(0, fields, 2):
        pair = [
            jnp.concatenate([y[pl.ds(f, half, stride=fields), :] for y in (own, other)], axis=0)
            for f in (field, field + 1)
        ]
        result = dot3(matrix, split(jnp.concatenate(pair, axis=1)))
        for i in range(2):
            for step, out in enumerate(outs):
                out[pl.ds(field + i, times, stride=fields), :] = result[
                    step * times : (step + 1) * times, i * PATCH : (i + 1) * PATCH
                ]


def geometry_body(cells, columns, rows, r_ref, static_ref):
    for patch in range(PATCH_DEV):
        targets = rows[:, patch * PATCH : (patch + 1) * PATCH]

        def slot(k, _):
            start = pl.multiple_of(cells[patch * NEAR_MOST + k] * PATCH, PATCH)
            sources = columns[pl.ds(start, PATCH), :]
            total = jnp.zeros((PATCH, PATCH), f32)
            for axis in range(3):
                gap = targets[axis : axis + 1, :] - sources[:, axis : axis + 1]
                total = total + gap * gap
            r = jnp.sqrt(total + smoothing * smoothing)
            r_ref[patch, k] = r
            static_ref[patch, k] = 1.0 / ((4.0 * np.pi) * r)
            return 0

        lax.fori_loop(0, NEAR_MOST, slot, 0)


def kernel_body(first, freqs, counts, rate, turns, r_ref, static_ref, out, held, sems):
    chunks = freqs // UNROLL
    live = counts[0] + counts[1]

    def copy(n, to):
        block, chunk = n // chunks, n % chunks
        patch = (block >= counts[0]).astype(jnp.int32)
        slot = block - patch * counts[0]
        target = out.at[patch, slot, pl.ds(chunk * UNROLL, UNROLL)]
        return pltpu.make_async_copy(held.at[to], target, sems.at[to])

    def step(n, _):
        to = n % 2
        block, chunk = n // chunks, n % chunks
        patch = (block >= counts[0]).astype(jnp.int32)
        slot = block - patch * counts[0]

        @pl.when(n >= 2)
        def _():
            copy(n - 2, to).wait()

        r, static_part = r_ref[patch, slot], static_ref[patch, slot]
        for u in range(UNROLL):
            at = first + chunk * UNROLL + u
            real, imag = kernel_value(r, static_part, rate[at], turns[at])
            for part, value in enumerate((real, imag)):
                high, low = split(value)
                held[to, u, 0, :, part * PATCH : (part + 1) * PATCH] = high
                held[to, u, 1, :, part * PATCH : (part + 1) * PATCH] = low
        copy(n, to).start()
        return 0

    total = live * chunks
    lax.fori_loop(0, total, step, 0)

    def drain(n, _):
        copy(n, n % 2).wait()
        return 0

    lax.fori_loop(jnp.maximum(total - 2, 0), total, drain, 0)


def near_body(fields, stored, freqs, counts, places, rate, turns, which, r_ref, static_ref, *refs):
    spectra, kernels = refs[:6], refs[6 : 6 + len(stored)]
    out, s_ref, held, s_sems, sems = refs[6 + len(stored) :]
    rows = 2 * fields
    patch = which[0]
    count = counts[patch]
    copies = [pltpu.make_async_copy(ref, s_ref.at[i], s_sems.at[i]) for i, ref in enumerate(spectra)]
    for c in copies:
        c.start()

    bounds = [0]
    for n in stored:
        bounds.append(bounds[-1] + n // UNROLL)
    stored_chunks, all_chunks = bounds[-1], freqs // UNROLL

    def copy(source, first_chunk, chunk, slot):
        to = chunk % 2
        return pltpu.make_async_copy(
            source.at[patch, slot, pl.ds((chunk - first_chunk) * UNROLL, UNROLL)],
            held.at[to, slot],
            sems.at[to, slot],
        )

    def fetch(chunk):
        for source, low, high in zip(kernels, bounds[:-1], bounds[1:]):

            @pl.when((chunk >= low) & (chunk < high))
            def _():
                def one(slot, _):
                    copy(source, low, chunk, slot).start()
                    return 0

                lax.fori_loop(0, count, one, 0)

    def spectrum(place, at):
        start = pl.multiple_of(at * rows, rows)
        return split(s_ref[place, pl.ds(start, rows), :])

    def finish(first, sums):
        for u, total in enumerate(sums):
            start = pl.multiple_of((first + u) * rows, rows)
            real = total[:fields, :PATCH] - total[fields:, PATCH:]
            imag = total[:fields, PATCH:] + total[fields:, :PATCH]
            out[pl.ds(start, rows), :] = jnp.concatenate([real, imag], axis=0)

    def product(spectrum_parts, kernel_parts):
        s_high, s_low = spectrum_parts
        k_high, k_low = kernel_parts
        both = dot(jnp.concatenate([s_high, s_low], axis=0), k_high)
        return both[:rows] + (both[rows:] + dot(s_high, k_low))

    zeros = tuple(jnp.zeros((rows, 2 * PATCH), f32) for _ in range(UNROLL))

    if stored_chunks:
        fetch(0)
        fetch(1)
    for c in copies:
        c.wait()

    def fresh(chunk, _):
        first = chunk * UNROLL

        def slot(k, sums):
            r, static_part = r_ref[patch, k], static_ref[patch, k]
            place = places[patch * NEAR_MOST + k]
            new = []
            for u in range(UNROLL):
                real, imag = kernel_value(r, static_part, rate[first + u], turns[first + u])
                (rh, rl), (ih, il) = split(real), split(imag)
                parts = jnp.concatenate([rh, ih], axis=1), jnp.concatenate([rl, il], axis=1)
                new.append(sums[u] + product(spectrum(place, first + u), parts))
            return tuple(new)

        finish(first, lax.fori_loop(0, count, slot, zeros))
        return 0

    lax.fori_loop(stored_chunks, all_chunks, fresh, 0)

    def ready(chunk, _):
        first = chunk * UNROLL
        to = chunk % 2

        def slot(k, sums):
            pltpu.make_async_copy(held.at[to, k], held.at[to, k], sems.at[to, k]).wait()
            place = places[patch * NEAR_MOST + k]
            new = []
            for u in range(UNROLL):
                parts = held[to, k, u, 0], held[to, k, u, 1]
                new.append(sums[u] + product(spectrum(place, first + u), parts))
            return tuple(new)

        finish(first, lax.fori_loop(0, count, slot, zeros))
        fetch(chunk + 2)
        return 0

    lax.fori_loop(0, stored_chunks, ready, 0)


def shift(x, axis, by):
    count = lax.axis_size(axis)
    return lax.ppermute(x, axis, [(i, (i + by) % count) for i in range(count)])


def fast_body(density, coords, weights, neighbours, counts):
    times, all_fields, width = density.shape
    parts = lax.axis_size("freq")
    node_parts = lax.axis_size("node")
    fields = all_fields * PATCH_DEV // parts
    freqs = STEPS // 4
    part = lax.axis_index("freq")
    half = part % 2
    where = jnp.stack([part, half]).astype(jnp.int32)
    block = shape(times * fields, PATCH)
    spectrum = shape(freqs * 2 * fields, PATCH)

    left, right = shift(coords, "node", 1), shift(coords, "node", -1)
    columns = jnp.concatenate([left, coords, right], axis=1).T
    total_patches = PATCH_DEV * node_parts
    first_patch = (lax.axis_index("node") - 1) * PATCH_DEV
    cells = jnp.clip((neighbours - first_patch) % total_patches, 0, 3 * PATCH_DEV - 1)
    cells = cells.reshape(PATCH_DEV * NEAR_MOST)
    owner, patch_at = cells // PATCH_DEV, cells % PATCH_DEV
    places = jnp.where(owner == 1, 0, jnp.where(owner == 0, 2, 4)) + (patch_at != half)
    places = places.astype(jnp.int32)
    rate, turns = (lax.dynamic_slice_in_dim(jnp.asarray(t), half * freqs, freqs) for t in laplace_table())

    sends = call(
        functools.partial(pack_body, parts, fields),
        "pack",
        [block] * parts,
        (where, density),
        [SMEM, VMEM],
        moved=density.size * 8,
    )
    blocks = [sends[0]] + [shift(sends[s], "freq", s) for s in range(1, parts)]

    pair_shape = shape(PATCH_DEV, NEAR_MOST, PATCH, PATCH)
    r, static_part = call(
        geometry_body,
        "geometry",
        [pair_shape] * 2,
        (cells, columns, coords),
        [SMEM, VMEM, VMEM],
        flops=PATCH_DEV * NEAR_MOST * PATCH * PATCH * 16,
        moved=PATCH_DEV * NEAR_MOST * PATCH * PATCH * 8,
    )

    def kernels(first, count):
        blocks_most = PATCH_DEV * NEAR_MOST * count
        return call(
            functools.partial(kernel_body, first, count),
            "kernels",
            shape(PATCH_DEV, NEAR_MOST, count, 2, PATCH, 2 * PATCH, dtype=bf16),
            (counts, rate, turns, r, static_part),
            [SMEM] * 3 + [VMEM] * 2,
            ANY,
            [
                pltpu.VMEM((2, UNROLL, 2, PATCH, 2 * PATCH), bf16),
                pltpu.SemaphoreType.DMA((2,)),
            ],
            flops=blocks_most * PATCH * PATCH * 32,
            moved=blocks_most * PATCH * PATCH * 8,
            trans=blocks_most * PATCH * PATCH,
        )

    stored = (freqs // 2, freqs // 4)
    first_kernels = kernels(0, stored[0])

    table = forward_table().reshape(parts, times, 2, STEPS // 2).transpose(0, 2, 3, 1)
    table = np.ascontiguousarray(table.transpose(0, 1, 3, 2))
    mine = lax.dynamic_slice_in_dim(weights, half * PATCH, PATCH).reshape(1, PATCH)
    own, other = call(
        functools.partial(forward_body, parts, fields),
        "forward",
        [spectrum] * 2,
        (where, jnp.asarray(table), mine, *blocks),
        [SMEM] + [VMEM] * (2 + parts),
        flops=6 * STEPS * STEPS * fields * PATCH,
        moved=STEPS * fields * PATCH * 8,
    )
    swap = [(i, i ^ 1) for i in range(parts)]
    paired = lax.ppermute(other, "freq", swap)
    own_left, own_right = shift(own, "node", 1), shift(own, "node", -1)
    second_kernels = kernels(stored[0], stored[1])
    paired_left, paired_right = shift(paired, "node", 1), shift(paired, "node", -1)

    def near(patch):
        return call(
            functools.partial(near_body, fields, stored, freqs),
            "near",
            spectrum,
            (
                counts, places, rate, turns, patch.reshape(1).astype(jnp.int32), r, static_part,
                own, paired, own_left, paired_left, own_right, paired_right,
                first_kernels, second_kernels,
            ),
            [SMEM] * 5 + [VMEM] * 2 + [ANY] * 8,
            VMEM,
            [
                pltpu.VMEM((6, freqs * 2 * fields, PATCH), f32),
                pltpu.VMEM((2, NEAR_MOST, UNROLL, 2, PATCH, 2 * PATCH), bf16),
                pltpu.SemaphoreType.DMA((6,)),
                pltpu.SemaphoreType.DMA((2, NEAR_MOST)),
            ],
            flops=freqs * NEAR_MOST * PATCH * PATCH * fields * 24,
            moved=freqs * NEAR_MOST * PATCH * PATCH * 8,
        )

    other_near = near(1 - half)
    got = lax.ppermute(other_near, "freq", swap)
    own_near = near(half)

    table = inverse_table().reshape(parts, times, 2, STEPS // 2).transpose(0, 2, 1, 3)
    outs = call(
        functools.partial(inverse_body, parts, fields),
        "inverse",
        [block] * parts,
        (where, jnp.asarray(np.ascontiguousarray(table)), own_near, got),
        [SMEM] + [VMEM] * 3,
        flops=6 * STEPS * STEPS * fields * PATCH,
        moved=STEPS * fields * PATCH * 8,
    )
    arrived = [outs[0]] + [shift(outs[s], "freq", s) for s in range(1, parts)]
    return call(
        functools.partial(unpack_body, parts, fields),
        "unpack",
        shape(times, all_fields, width),
        (where, *arrived),
        [SMEM] + [VMEM] * parts,
        moved=density.size * 8,
    )


def padded_2(cells, sides, width):
    for axis, dim in sides:
        count = lax.axis_size(axis)
        head = lax.slice_in_dim(cells, 0, width, axis=dim)
        tail = lax.slice_in_dim(cells, cells.shape[dim] - width, cells.shape[dim], axis=dim)
        cells = jnp.concatenate(
            [
                lax.ppermute(tail, axis, [(i, (i + 1) % count) for i in range(count)]),
                cells,
                lax.ppermute(head, axis, [((i + 1) % count, i) for i in range(count)]),
            ],
            axis=dim,
        )
    return cells


def fourier_tables(freq_count):
    freq_index = jnp.arange(freq_count, dtype=jnp.int32)
    time_index = jnp.arange(STEPS, dtype=jnp.int32)
    phase_index = (2 * freq_index[:, None] + 1) * time_index[None, :] % (2 * STEPS)
    phase_angle = phase_index.astype(jnp.float32) * (jnp.pi / STEPS)
    return (jnp.cos(phase_angle), jnp.sin(phase_angle))


def laplace_values(freq_index):
    phase_angle = (2 * freq_index + 1).astype(jnp.float32) * (jnp.pi / STEPS)
    radius = decay_ratio ** (1.0 / STEPS)
    offset_real = 1.0 - radius * jnp.cos(phase_angle)
    offset_imag = -radius * jnp.sin(phase_angle)
    delta_real = offset_real + 0.5 * (offset_real * offset_real - offset_imag * offset_imag)
    delta_imag = offset_imag + offset_real * offset_imag
    return (delta_real / time_step, delta_imag / time_step)


def time_weights(time_index, sign):
    radius = decay_ratio ** (1.0 / STEPS)
    return jnp.power(jnp.float32(radius), sign * time_index.astype(jnp.float32))


def kernel_terms(distance, static_part, value_real, value_imag):
    decaying = jnp.exp(-value_real * distance) * static_part
    return (decaying * jnp.cos(value_imag * distance), -decaying * jnp.sin(value_imag * distance))


def plain_body(density, coords, weights, neighbours, counts):
    local_times = density.shape[0]
    fields_here = density.shape[1]
    width = density.shape[2]
    freq_parts = lax.axis_size("freq")
    node_parts = lax.axis_size("node")
    spectrum_count = STEPS // 2
    factor = 2.0
    cosine, sine = fourier_tables(spectrum_count)
    own_times = lax.axis_index("freq") * local_times + jnp.arange(local_times, dtype=jnp.int32)
    scaled = density * time_weights(own_times, 1.0)[:, None, None]
    gathered_block = lax.all_to_all(scaled, "freq", split_axis=2, concat_axis=0, tiled=True)
    item_count = gathered_block.shape[1]
    column_count = gathered_block.shape[2]
    flattened = gathered_block.reshape(STEPS, item_count * column_count)
    part_real = jnp.dot(cosine, flattened, precision=highest, preferred_element_type=jnp.float32)
    part_imag = jnp.dot(sine, flattened, precision=highest, preferred_element_type=jnp.float32)
    spectrum = jnp.stack([part_real, part_imag], axis=1).reshape(
        spectrum_count, 2, item_count, column_count
    )
    own_spectrum = lax.all_to_all(spectrum, "freq", split_axis=0, concat_axis=3, tiled=True)
    local_freqs = spectrum_count // freq_parts
    rows_spec = local_freqs * 2 * fields_here
    packed = jnp.concatenate(
        [own_spectrum.reshape(rows_spec, width), coords, weights[None, :]], axis=0
    )
    padded = padded_2(packed, (("node", 1),), width)
    total_patches = PATCH_DEV * node_parts
    first_patch = (lax.axis_index("node") - 1) * PATCH_DEV
    local_slots = (neighbours - first_patch) % total_patches
    columns = (
        local_slots[:, :, None] * PATCH + jnp.arange(PATCH, dtype=jnp.int32)[None, None, :]
    ).reshape(PATCH_DEV, NEAR_MOST * PATCH)
    geometry = padded[rows_spec:]
    other_coords = geometry[:3][:, columns]
    live_slots = (jnp.arange(NEAR_MOST, dtype=jnp.int32)[None, :] < counts[:, None]).astype(
        jnp.float32
    )
    node_scale = geometry[3][columns] * jnp.repeat(live_slots, PATCH, axis=1)
    own_coords = coords.reshape(3, PATCH_DEV, PATCH)
    separation = own_coords[:, :, :, None] - other_coords[:, :, None, :]
    distance = jnp.sqrt(jnp.sum(separation * separation, axis=0) + smoothing * smoothing)
    static_part = node_scale[:, None, :] / (4.0 * jnp.pi * distance)
    spectra = padded[:rows_spec].reshape(local_freqs, 2, fields_here, 3 * width)
    freq_index = lax.axis_index("freq") * local_freqs + jnp.arange(local_freqs, dtype=jnp.int32)
    laplace_real, laplace_imag = laplace_values(freq_index)

    def one_freq(arguments):
        value_real, value_imag, freq_block = arguments
        picked = freq_block[:, :, columns]
        kern_real, kern_imag = kernel_terms(distance, static_part, value_real, value_imag)
        out_real = jnp.einsum("pij,rpj->rpi", kern_real, picked[0], precision=highest) - jnp.einsum(
            "pij,rpj->rpi", kern_imag, picked[1], precision=highest
        )
        out_imag = jnp.einsum("pij,rpj->rpi", kern_real, picked[1], precision=highest) + jnp.einsum(
            "pij,rpj->rpi", kern_imag, picked[0], precision=highest
        )
        return jnp.stack([out_real, out_imag]).reshape(2, fields_here, width)

    near_field = lax.map(one_freq, (laplace_real, laplace_imag, spectra))
    gathered_block = lax.all_to_all(near_field, "freq", split_axis=3, concat_axis=0, tiled=True)
    item_count = gathered_block.shape[2]
    column_count = gathered_block.shape[3]
    block_real = gathered_block[:, 0].reshape(spectrum_count, item_count * column_count)
    block_imag = gathered_block[:, 1].reshape(spectrum_count, item_count * column_count)
    summed = jnp.dot(
        cosine.T, block_real, precision=highest, preferred_element_type=jnp.float32
    ) + jnp.dot(sine.T, block_imag, precision=highest, preferred_element_type=jnp.float32)
    all_times = jnp.arange(STEPS, dtype=jnp.int32)
    summed = summed * (factor / STEPS) * time_weights(all_times, -1.0)[:, None]
    time_domain = summed.reshape(STEPS, item_count, column_count)
    return lax.all_to_all(time_domain, "freq", split_axis=0, concat_axis=2, tiled=True)


def body(density, coords, weights, neighbours, counts):
    parts = lax.axis_size("freq")
    fields = density.shape[1] * PATCH_DEV // parts
    whole = fields * parts == density.shape[1] * PATCH_DEV and fields % 8 == 0 and parts % 2 == 0
    if whole and density.shape[2] == PATCH_DEV * PATCH and density.shape[0] % 8 == 0:
        return fast_body(density, coords, weights, neighbours, counts)
    return plain_body(density, coords, weights, neighbours, counts)


def solution(mesh):
    placed = (P("freq", None, "node"), P(None, "node"), P("node"), P("node", None), P("node"))
    return jax.shard_map(
        body, mesh=mesh, in_specs=placed, out_specs=P("freq", None, "node"), check_vma=False
    )
```

```python
import functools

import jax
import jax.numpy as jnp
import numpy as np
from jax import lax
from jax.experimental import pallas as pl
from jax.experimental.pallas import tpu as pltpu
from jax.sharding import PartitionSpec as P

STEPS = 256
PATCH = 128
PATCH_DEV = 2
NEAR_MOST = 4

decay_ratio = 0.1
time_step = 1.0
smoothing = 0.5
highest = lax.Precision.HIGHEST

UNROLL = 8
f32 = jnp.float32
bf16 = jnp.bfloat16


def angles(freqs, times):
    phase = (2 * freqs[:, None] + 1) * times[None, :] % (2 * STEPS)
    return phase * (np.pi / STEPS)


def forward_table():
    times = np.arange(STEPS)
    angle = angles(np.arange(STEPS // 2), times)
    rows = np.stack([np.cos(angle), np.sin(angle)], axis=1).reshape(STEPS, STEPS)
    return (rows * decay_ratio ** (times / STEPS)).T.astype(np.float32)


def inverse_table():
    times = np.arange(STEPS)
    angle = angles(np.arange(STEPS // 2), times)
    rows = np.stack([np.cos(angle), np.sin(angle)], axis=1).reshape(STEPS, STEPS)
    return (rows.T * (2.0 / STEPS) * decay_ratio ** (-times[:, None] / STEPS)).astype(np.float32)


def laplace_table():
    zeta = decay_ratio ** (1.0 / STEPS) * np.exp(1j * np.pi * (2 * np.arange(STEPS // 2) + 1) / STEPS)
    value = ((1 - zeta) + (1 - zeta) ** 2 / 2) / time_step
    return (
        (-value.real / np.log(2.0)).astype(np.float32),
        (value.imag / (2 * np.pi)).astype(np.float32),
    )


def trig_series():
    w = 0.125 * (1 - np.cos(np.pi * (np.arange(4000) + 0.5) / 4000))

    def fit(values):
        basis = np.polynomial.chebyshev.chebvander(w * 8 - 1, 4)
        found = np.linalg.lstsq(basis, values, rcond=None)[0]
        series = np.polynomial.chebyshev.Chebyshev(found, domain=[0, 0.25])
        return [float(np.float32(c)) for c in series.convert(kind=np.polynomial.Polynomial).coef]

    root = np.sqrt(w)
    return (
        fit(np.sqrt(2.0) * np.sin(np.pi * root) / root),
        fit(np.sqrt(2.0) * np.cos(np.pi * root)),
    )


SINE, COSINE = trig_series()


def series(terms, w):
    total = terms[-1] * w + terms[-2]
    for term in terms[-3::-1]:
        total = total * w + term
    return total


def split(x):
    high = x.astype(bf16)
    return high, (x - high.astype(f32)).astype(bf16)


def dot(a, b):
    return jnp.dot(a, b, preferred_element_type=f32)


def dot3(a, b):
    (a_high, a_low), (b_high, b_low) = a, b
    return dot(a_high, b_high) + (dot(a_high, b_low) + dot(a_low, b_high))


def kernel_value(r, static_part, rate, turns):
    t = r * turns
    u = t - jnp.round(t)
    w = u * u
    s = series(SINE, w) * u
    c = series(COSINE, w)
    e = jnp.exp2(r * rate) * static_part
    es = e * s
    return e - es * s, -(es * c)


VMEM = pl.BlockSpec(memory_space=pltpu.VMEM)
SMEM = pl.BlockSpec(memory_space=pltpu.SMEM)
ANY = pl.BlockSpec(memory_space=pl.ANY)


def call(body, name, outs, ins, specs, out_specs=None, scratch=(), flops=0, moved=0, trans=0):
    return pl.pallas_call(
        body,
        name=name,
        out_shape=outs,
        in_specs=specs,
        out_specs=out_specs if out_specs is not None else jax.tree.map(lambda _: VMEM, outs),
        scratch_shapes=list(scratch),
        cost_estimate=pl.CostEstimate(flops=flops, bytes_accessed=moved, transcendentals=trans),
    )(*ins)


def shape(*dims, dtype=f32):
    return jax.ShapeDtypeStruct(dims, dtype)


def pack_body(parts, fields, x_ref, *outs):
    times = x_ref.shape[0]
    part = lax.axis_index("freq")
    for step, out in enumerate(outs):
        group = lax.rem(part + step, parts)
        field0 = pl.multiple_of(group // 2 * fields, 8)
        node0 = pl.multiple_of(group % 2 * PATCH, PATCH)
        block = x_ref[:, pl.ds(field0, fields), pl.ds(node0, PATCH)]
        out[...] = block.reshape(times * fields, PATCH)


def unpack_body(parts, fields, *refs):
    out = refs[-1]
    times = out.shape[0]
    part = lax.axis_index("freq")
    for step, ref in enumerate(refs[:-1]):
        group = lax.rem(part + parts - step, parts)
        field0 = pl.multiple_of(group // 2 * fields, 8)
        node0 = pl.multiple_of(group % 2 * PATCH, PATCH)
        out[:, pl.ds(field0, fields), pl.ds(node0, PATCH)] = ref[...].reshape(times, fields, PATCH)


def own_half_first(rows, axis):
    low_half = lax.rem(lax.axis_index("freq"), 2) == 0
    first = jnp.where(low_half, rows[0], rows[1])
    second = jnp.where(low_half, rows[1], rows[0])
    return jnp.concatenate([first, second], axis=axis)


def forward_body(parts, fields, table, weights, *refs):
    blocks, (own, other) = refs[:parts], refs[-2:]
    times = STEPS // parts
    half = STEPS // 2
    part = lax.axis_index("freq")
    rows = jnp.concatenate(
        [table[lax.rem(part + parts - step, parts)] for step in range(parts)], axis=1
    )
    matrix = split(own_half_first(rows, 1).T)
    scale = jnp.where(lax.rem(part, 2) == 0, weights[:, :PATCH], weights[:, PATCH:])
    for field in range(0, fields, 2):
        pair = [
            jnp.concatenate([b[pl.ds(f, times, stride=fields), :] for b in blocks], axis=0)
            for f in (field, field + 1)
        ]
        result = dot3(matrix, split(jnp.concatenate(pair, axis=1)))
        for i in range(2):
            column = result[:, i * PATCH : (i + 1) * PATCH] * scale
            own[pl.ds(field + i, half, stride=fields), :] = column[:half]
            other[pl.ds(field + i, half, stride=fields), :] = column[half:]


def inverse_body(parts, fields, table, own, other, *outs):
    times = STEPS // parts
    half = STEPS // 2
    part = lax.axis_index("freq")
    matrix = split(
        jnp.concatenate(
            [own_half_first(table[lax.rem(part + step, parts)], 1) for step in range(parts)], axis=0
        )
    )
    for field in range(0, fields, 2):
        pair = [
            jnp.concatenate([y[pl.ds(f, half, stride=fields), :] for y in (own, other)], axis=0)
            for f in (field, field + 1)
        ]
        result = dot3(matrix, split(jnp.concatenate(pair, axis=1)))
        for i in range(2):
            for step, out in enumerate(outs):
                out[pl.ds(field + i, times, stride=fields), :] = result[
                    step * times : (step + 1) * times, i * PATCH : (i + 1) * PATCH
                ]


def cell_of(neighbours, patch, slot):
    total = PATCH_DEV * lax.axis_size("node")
    first = (lax.axis_index("node") - 1) * PATCH_DEV
    cell = lax.rem(neighbours[patch, slot] - first + total, total)
    return jnp.minimum(cell, 3 * PATCH_DEV - 1)


def place_of(neighbours, patch, slot):
    cell = cell_of(neighbours, patch, slot)
    owner, at = cell // PATCH_DEV, lax.rem(cell, PATCH_DEV)
    base = jnp.where(owner == 1, 0, jnp.where(owner == 0, 2, 4))
    return base + (at != lax.rem(lax.axis_index("freq"), 2)).astype(jnp.int32)


def geometry_body(neighbours, left, here, right, r_ref, static_ref, columns):
    for owner, ref in enumerate((left, here, right)):
        for patch in range(PATCH_DEV):
            rows = ref[:, patch * PATCH : (patch + 1) * PATCH]
            padded = jnp.concatenate([rows, jnp.zeros((5, PATCH), f32)], axis=0)
            columns[owner * PATCH_DEV + patch] = padded.T
    for patch in range(PATCH_DEV):
        targets = here[:, patch * PATCH : (patch + 1) * PATCH]

        def slot(k, _):
            sources = columns[cell_of(neighbours, patch, k)]
            total = jnp.zeros((PATCH, PATCH), f32)
            for axis in range(3):
                gap = targets[axis : axis + 1, :] - sources[:, axis : axis + 1]
                total = total + gap * gap
            r = jnp.sqrt(total + smoothing * smoothing)
            r_ref[patch, k] = r
            static_ref[patch, k] = 1.0 / ((4.0 * np.pi) * r)
            return 0

        lax.fori_loop(0, NEAR_MOST, slot, 0)


def kernel_body(first, freqs, counts, rate, turns, r_ref, static_ref, *refs):
    out, held, sems = refs[-3:]
    chunks = freqs // UNROLL
    live = counts[0] + counts[1]
    base = lax.rem(lax.axis_index("freq"), 2) * (STEPS // 4) + first

    def place(n):
        block, chunk = n // chunks, lax.rem(n, chunks)
        patch = (block >= counts[0]).astype(jnp.int32)
        return patch, block - patch * counts[0], chunk

    def copy(n, to):
        patch, slot, chunk = place(n)
        target = out.at[patch, slot, pl.ds(chunk * UNROLL, UNROLL)]
        return pltpu.make_async_copy(held.at[to], target, sems.at[to])

    def step(n, _):
        to = lax.rem(n, 2)
        patch, slot, chunk = place(n)

        @pl.when(n >= 2)
        def _():
            copy(n - 2, to).wait()

        r, static_part = r_ref[patch, slot], static_ref[patch, slot]
        for u in range(UNROLL):
            at = base + chunk * UNROLL + u
            real, imag = kernel_value(r, static_part, rate[at], turns[at])
            for part, value in enumerate((real, imag)):
                high, low = split(value)
                held[to, u, 0, :, part * PATCH : (part + 1) * PATCH] = high
                held[to, u, 1, :, part * PATCH : (part + 1) * PATCH] = low
        copy(n, to).start()
        return 0

    total = live * chunks
    lax.fori_loop(0, total, step, 0)

    def drain(n, _):
        copy(n, lax.rem(n, 2)).wait()
        return 0

    lax.fori_loop(jnp.maximum(total - 2, 0), total, drain, 0)


def near_body(fields, stored, freqs, mine, counts, neighbours, rate, turns, r_ref, static_ref, *refs):
    spectra, kernels = refs[:6], refs[6 : 6 + len(stored)]
    out, s_ref, held, s_sems, sems = refs[6 + len(stored) :]
    rows = 2 * fields
    half = lax.rem(lax.axis_index("freq"), 2)
    base = half * (STEPS // 4)
    patch = half if mine else 1 - half
    count = counts[patch]
    copies = [pltpu.make_async_copy(ref, s_ref.at[i], s_sems.at[i]) for i, ref in enumerate(spectra)]
    for c in copies:
        c.start()

    bounds = [0]
    for n in stored:
        bounds.append(bounds[-1] + n // UNROLL)
    stored_chunks, all_chunks = bounds[-1], freqs // UNROLL

    def fetch(chunk):
        to = lax.rem(chunk, 2)
        for source, low, high in zip(kernels, bounds[:-1], bounds[1:]):

            @pl.when((chunk >= low) & (chunk < high))
            def _():
                def one(slot, _):
                    pltpu.make_async_copy(
                        source.at[patch, slot, pl.ds((chunk - low) * UNROLL, UNROLL)],
                        held.at[to, slot],
                        sems.at[to, slot],
                    ).start()
                    return 0

                lax.fori_loop(0, count, one, 0)

    def spectrum(place, at):
        start = pl.multiple_of(at * rows, rows)
        return split(s_ref[place, pl.ds(start, rows), :])

    def finish(first, sums):
        for u, total in enumerate(sums):
            start = pl.multiple_of((first + u) * rows, rows)
            real = total[:fields, :PATCH] - total[fields:, PATCH:]
            imag = total[:fields, PATCH:] + total[fields:, :PATCH]
            out[pl.ds(start, rows), :] = jnp.concatenate([real, imag], axis=0)

    def product(spectrum_parts, kernel_parts):
        s_high, s_low = spectrum_parts
        k_high, k_low = kernel_parts
        both = dot(jnp.concatenate([s_high, s_low], axis=0), k_high)
        return both[:rows] + (both[rows:] + dot(s_high, k_low))

    zeros = tuple(jnp.zeros((rows, 2 * PATCH), f32) for _ in range(UNROLL))

    fetch(0)
    fetch(1)
    for c in copies:
        c.wait()

    def fresh(chunk, _):
        first = chunk * UNROLL

        def slot(k, sums):
            r, static_part = r_ref[patch, k], static_ref[patch, k]
            place = place_of(neighbours, patch, k)
            new = []
            for u in range(UNROLL):
                at = first + u
                real, imag = kernel_value(r, static_part, rate[base + at], turns[base + at])
                (rh, rl), (ih, il) = split(real), split(imag)
                parts = jnp.concatenate([rh, ih], axis=1), jnp.concatenate([rl, il], axis=1)
                new.append(sums[u] + product(spectrum(place, at), parts))
            return tuple(new)

        finish(first, lax.fori_loop(0, count, slot, zeros))
        return 0

    if stored_chunks < all_chunks:
        lax.fori_loop(stored_chunks, all_chunks, fresh, 0)

    def ready(chunk, _):
        first = chunk * UNROLL
        to = lax.rem(chunk, 2)

        def slot(k, sums):
            pltpu.make_async_copy(held.at[to, k], held.at[to, k], sems.at[to, k]).wait()
            place = place_of(neighbours, patch, k)
            new = []
            for u in range(UNROLL):
                parts = held[to, k, u, 0], held[to, k, u, 1]
                new.append(sums[u] + product(spectrum(place, first + u), parts))
            return tuple(new)

        finish(first, lax.fori_loop(0, count, slot, zeros))
        fetch(chunk + 2)
        return 0

    lax.fori_loop(0, stored_chunks, ready, 0)


def shift(x, axis, by):
    count = lax.axis_size(axis)
    return lax.ppermute(x, axis, [(i, (i + by) % count) for i in range(count)])


STORED = (24, 16, 8)


def fast_body(density, coords, weights, neighbours, counts):
    times, all_fields, width = density.shape
    parts = lax.axis_size("freq")
    fields = all_fields * PATCH_DEV // parts
    freqs = STEPS // 4
    block = shape(times * fields, PATCH)
    spectrum = shape(freqs * 2 * fields, PATCH)
    rate, turns = (jnp.asarray(t) for t in laplace_table())
    swap = [(i, i ^ 1) for i in range(parts)]

    left, right = shift(coords, "node", 1), shift(coords, "node", -1)
    pair_shape = shape(PATCH_DEV, NEAR_MOST, PATCH, PATCH)
    r, static_part = call(
        geometry_body,
        "geometry",
        [pair_shape] * 2,
        (neighbours, left, coords, right),
        [SMEM] + [VMEM] * 3,
        scratch=[pltpu.VMEM((3 * PATCH_DEV, PATCH, 8), f32)],
        flops=PATCH_DEV * NEAR_MOST * PATCH * PATCH * 16,
        moved=PATCH_DEV * NEAR_MOST * PATCH * PATCH * 8,
    )

    sends = call(
        functools.partial(pack_body, parts, fields),
        "pack",
        [block] * parts,
        (density,),
        [VMEM],
        moved=density.size * 8,
    )
    blocks = [sends[0]] + [shift(sends[s], "freq", s) for s in range(1, parts)]

    def kernels(first, count, after):
        blocks_most = PATCH_DEV * NEAR_MOST * count
        return call(
            functools.partial(kernel_body, first, count),
            "kernels",
            shape(PATCH_DEV, NEAR_MOST, count, 2, PATCH, 2 * PATCH, dtype=bf16),
            (counts, rate, turns, r, static_part, *after),
            [SMEM] * 3 + [VMEM] * 2 + [ANY] * len(after),
            ANY,
            [
                pltpu.VMEM((2, UNROLL, 2, PATCH, 2 * PATCH), bf16),
                pltpu.SemaphoreType.DMA((2,)),
            ],
            flops=blocks_most * PATCH * PATCH * 32,
            moved=blocks_most * PATCH * PATCH * 8,
            trans=blocks_most * PATCH * PATCH,
        )

    first_kernels = kernels(0, STORED[0], ())

    table = forward_table().reshape(parts, times, 2, STEPS // 2).transpose(0, 2, 1, 3)
    own, other = call(
        functools.partial(forward_body, parts, fields),
        "forward",
        [spectrum] * 2,
        (jnp.asarray(np.ascontiguousarray(table)), weights.reshape(1, width), *blocks, first_kernels),
        [VMEM] * (2 + parts) + [ANY],
        flops=6 * STEPS * STEPS * fields * PATCH,
        moved=STEPS * fields * PATCH * 8,
    )
    paired = lax.ppermute(other, "freq", swap)
    own_left, own_right = shift(own, "node", 1), shift(own, "node", -1)
    second_kernels = kernels(STORED[0], STORED[1], (own,))
    paired, second_kernels = lax.optimization_barrier((paired, second_kernels))
    paired_left, paired_right = shift(paired, "node", 1), shift(paired, "node", -1)
    third_kernels = kernels(STORED[0] + STORED[1], STORED[2], (paired, second_kernels))

    def near(mine):
        return call(
            functools.partial(near_body, fields, STORED, freqs, mine),
            "near",
            spectrum,
            (
                counts, neighbours, rate, turns, r, static_part,
                own, paired, own_left, paired_left, own_right, paired_right,
                first_kernels, second_kernels, third_kernels,
            ),
            [SMEM] * 4 + [VMEM] * 2 + [ANY] * 9,
            VMEM,
            [
                pltpu.VMEM((6, freqs * 2 * fields, PATCH), f32),
                pltpu.VMEM((2, NEAR_MOST, UNROLL, 2, PATCH, 2 * PATCH), bf16),
                pltpu.SemaphoreType.DMA((6,)),
                pltpu.SemaphoreType.DMA((2, NEAR_MOST)),
            ],
            flops=freqs * NEAR_MOST * PATCH * PATCH * fields * 24,
            moved=freqs * NEAR_MOST * PATCH * PATCH * 8,
        )

    got = lax.ppermute(near(False), "freq", swap)
    own_near = near(True)

    table = inverse_table().reshape(parts, times, 2, STEPS // 2).transpose(0, 2, 1, 3)
    outs = call(
        functools.partial(inverse_body, parts, fields),
        "inverse",
        [block] * parts,
        (jnp.asarray(np.ascontiguousarray(table)), own_near, got),
        [VMEM] * 3,
        flops=6 * STEPS * STEPS * fields * PATCH,
        moved=STEPS * fields * PATCH * 8,
    )
    arrived = [outs[0]] + [shift(outs[s], "freq", s) for s in range(1, parts)]
    return call(
        functools.partial(unpack_body, parts, fields),
        "unpack",
        shape(times, all_fields, width),
        tuple(arrived),
        [VMEM] * parts,
        moved=density.size * 8,
    )


def padded_2(cells, sides, width):
    for axis, dim in sides:
        count = lax.axis_size(axis)
        head = lax.slice_in_dim(cells, 0, width, axis=dim)
        tail = lax.slice_in_dim(cells, cells.shape[dim] - width, cells.shape[dim], axis=dim)
        cells = jnp.concatenate(
            [
                lax.ppermute(tail, axis, [(i, (i + 1) % count) for i in range(count)]),
                cells,
                lax.ppermute(head, axis, [((i + 1) % count, i) for i in range(count)]),
            ],
            axis=dim,
        )
    return cells


def fourier_tables(freq_count):
    freq_index = jnp.arange(freq_count, dtype=jnp.int32)
    time_index = jnp.arange(STEPS, dtype=jnp.int32)
    phase_index = (2 * freq_index[:, None] + 1) * time_index[None, :] % (2 * STEPS)
    phase_angle = phase_index.astype(jnp.float32) * (jnp.pi / STEPS)
    return (jnp.cos(phase_angle), jnp.sin(phase_angle))


def laplace_values(freq_index):
    phase_angle = (2 * freq_index + 1).astype(jnp.float32) * (jnp.pi / STEPS)
    radius = decay_ratio ** (1.0 / STEPS)
    offset_real = 1.0 - radius * jnp.cos(phase_angle)
    offset_imag = -radius * jnp.sin(phase_angle)
    delta_real = offset_real + 0.5 * (offset_real * offset_real - offset_imag * offset_imag)
    delta_imag = offset_imag + offset_real * offset_imag
    return (delta_real / time_step, delta_imag / time_step)


def time_weights(time_index, sign):
    radius = decay_ratio ** (1.0 / STEPS)
    return jnp.power(jnp.float32(radius), sign * time_index.astype(jnp.float32))


def kernel_terms(distance, static_part, value_real, value_imag):
    decaying = jnp.exp(-value_real * distance) * static_part
    return (decaying * jnp.cos(value_imag * distance), -decaying * jnp.sin(value_imag * distance))


def plain_body(density, coords, weights, neighbours, counts):
    local_times = density.shape[0]
    fields_here = density.shape[1]
    width = density.shape[2]
    freq_parts = lax.axis_size("freq")
    node_parts = lax.axis_size("node")
    spectrum_count = STEPS // 2
    factor = 2.0
    cosine, sine = fourier_tables(spectrum_count)
    own_times = lax.axis_index("freq") * local_times + jnp.arange(local_times, dtype=jnp.int32)
    scaled = density * time_weights(own_times, 1.0)[:, None, None]
    gathered_block = lax.all_to_all(scaled, "freq", split_axis=2, concat_axis=0, tiled=True)
    item_count = gathered_block.shape[1]
    column_count = gathered_block.shape[2]
    flattened = gathered_block.reshape(STEPS, item_count * column_count)
    part_real = jnp.dot(cosine, flattened, precision=highest, preferred_element_type=jnp.float32)
    part_imag = jnp.dot(sine, flattened, precision=highest, preferred_element_type=jnp.float32)
    spectrum = jnp.stack([part_real, part_imag], axis=1).reshape(
        spectrum_count, 2, item_count, column_count
    )
    own_spectrum = lax.all_to_all(spectrum, "freq", split_axis=0, concat_axis=3, tiled=True)
    local_freqs = spectrum_count // freq_parts
    rows_spec = local_freqs * 2 * fields_here
    packed = jnp.concatenate(
        [own_spectrum.reshape(rows_spec, width), coords, weights[None, :]], axis=0
    )
    padded = padded_2(packed, (("node", 1),), width)
    total_patches = PATCH_DEV * node_parts
    first_patch = (lax.axis_index("node") - 1) * PATCH_DEV
    local_slots = (neighbours - first_patch) % total_patches
    columns = (
        local_slots[:, :, None] * PATCH + jnp.arange(PATCH, dtype=jnp.int32)[None, None, :]
    ).reshape(PATCH_DEV, NEAR_MOST * PATCH)
    geometry = padded[rows_spec:]
    other_coords = geometry[:3][:, columns]
    live_slots = (jnp.arange(NEAR_MOST, dtype=jnp.int32)[None, :] < counts[:, None]).astype(
        jnp.float32
    )
    node_scale = geometry[3][columns] * jnp.repeat(live_slots, PATCH, axis=1)
    own_coords = coords.reshape(3, PATCH_DEV, PATCH)
    separation = own_coords[:, :, :, None] - other_coords[:, :, None, :]
    distance = jnp.sqrt(jnp.sum(separation * separation, axis=0) + smoothing * smoothing)
    static_part = node_scale[:, None, :] / (4.0 * jnp.pi * distance)
    spectra = padded[:rows_spec].reshape(local_freqs, 2, fields_here, 3 * width)
    freq_index = lax.axis_index("freq") * local_freqs + jnp.arange(local_freqs, dtype=jnp.int32)
    laplace_real, laplace_imag = laplace_values(freq_index)

    def one_freq(arguments):
        value_real, value_imag, freq_block = arguments
        picked = freq_block[:, :, columns]
        kern_real, kern_imag = kernel_terms(distance, static_part, value_real, value_imag)
        out_real = jnp.einsum("pij,rpj->rpi", kern_real, picked[0], precision=highest) - jnp.einsum(
            "pij,rpj->rpi", kern_imag, picked[1], precision=highest
        )
        out_imag = jnp.einsum("pij,rpj->rpi", kern_real, picked[1], precision=highest) + jnp.einsum(
            "pij,rpj->rpi", kern_imag, picked[0], precision=highest
        )
        return jnp.stack([out_real, out_imag]).reshape(2, fields_here, width)

    near_field = lax.map(one_freq, (laplace_real, laplace_imag, spectra))
    gathered_block = lax.all_to_all(near_field, "freq", split_axis=3, concat_axis=0, tiled=True)
    item_count = gathered_block.shape[2]
    column_count = gathered_block.shape[3]
    block_real = gathered_block[:, 0].reshape(spectrum_count, item_count * column_count)
    block_imag = gathered_block[:, 1].reshape(spectrum_count, item_count * column_count)
    summed = jnp.dot(
        cosine.T, block_real, precision=highest, preferred_element_type=jnp.float32
    ) + jnp.dot(sine.T, block_imag, precision=highest, preferred_element_type=jnp.float32)
    all_times = jnp.arange(STEPS, dtype=jnp.int32)
    summed = summed * (factor / STEPS) * time_weights(all_times, -1.0)[:, None]
    time_domain = summed.reshape(STEPS, item_count, column_count)
    return lax.all_to_all(time_domain, "freq", split_axis=0, concat_axis=2, tiled=True)


def body(density, coords, weights, neighbours, counts):
    parts = lax.axis_size("freq")
    fields = density.shape[1] * PATCH_DEV // parts
    whole = fields * parts == density.shape[1] * PATCH_DEV and fields % 8 == 0 and parts % 2 == 0
    if whole and density.shape[2] == PATCH_DEV * PATCH and density.shape[0] % 8 == 0:
        return fast_body(density, coords, weights, neighbours, counts)
    return plain_body(density, coords, weights, neighbours, counts)


def solution(mesh):
    placed = (P("freq", None, "node"), P(None, "node"), P("node"), P("node", None), P("node"))
    return jax.shard_map(
        body, mesh=mesh, in_specs=placed, out_specs=P("freq", None, "node"), check_vma=False
    )
```
